128 devices in a mesh: dp: 8 (over y, core), expert: 16 (over z, x).
Axes of the slice: x: 4, y: 4, z: 4, core: 2. Of those that a mesh axis runs over, the one named last changes fastest.
Arguments:
- tokens: bfloat16 [32768, 2048], P(('dp', 'expert')), parts along dimension 0, may hold values from -6 to 6
- target: int32 [32768, 8], P(('dp', 'expert')), parts along dimension 0, may hold values from 0 to 47, as said below
- router_weight: float32 [32768, 8], P(('dp', 'expert')), parts along dimension 0, may hold values from 0.1 to 1
- replica_pick: int32 [128], P(('dp', 'expert')), parts along dimension 0, may hold values from 0 to 1
- w_gate: bfloat16 [32, 2048, 768], P('expert'), may hold values from -0.125 to 0.125
- w_up: bfloat16 [32, 2048, 768], P('expert'), may hold values from -0.125 to 0.125
- w_down: bfloat16 [32, 768, 2048], P('expert'), may hold values from -0.21875 to 0.21875
Outputs:
- mixed: bfloat16 [32768, 2048], P(('dp', 'expert')), parts along dimension 0
The draws below stay inside these ranges and needn't reach their ends.
There are 8 independent parts, one for each index of `dp`. The reference program is written for one: setup_inputs(seed, part) draws one part's arguments, and reference() takes and returns one part's arrays. A program takes and returns all parts, laid end to end along the dimension named above; an argument that names none is the same for every part. Nothing has to cross between parts.
Inputs may be any that keep to these rules, and one draw needn't show every extreme that they name: `target`: within each aligned block of 256 rows (one device's tokens) no slot is named more than 64 times, and at least one slot, the same one in every block, is named exactly 64 times in every block (other slots may also reach 64); the 8 slots of a row name 8 different experts.
All inputs are finite; a program needn't handle non-finite values.
Results may differ from the reference program's by a relative error of at most 0.008.
Values may be sent and summed in bfloat16 or wider, within the bound.
A program may use at most 192 MiB of HBM per device.

```python
import math
import jax
import jax.numpy as jnp
from jax import lax

D = 2048
FF = 768
TOP = 8
EXP_DEV = 2
TOK_DEV = 256
EXPERTS = 32
TOKENS = 4096
CAP = 64
N_EXPERT = 16


def lent_choices(key):
    return jax.random.randint(jax.random.fold_in(key, 11), (N_EXPERT,), 0, EXP_DEV).astype(jnp.int32)


def draw_replica_pick(key, part):
    return lent_choices(key)


def draw_target(key, part):
    pick = lent_choices(key)
    slots = EXP_DEV + 1
    virtual = N_EXPERT * slots
    labels = jnp.arange(virtual, dtype=jnp.int32)
    hosts = labels // slots
    local = labels % slots
    left = (hosts - 1) % N_EXPERT
    order_key = jnp.where(local < EXP_DEV, 2 * (hosts * EXP_DEV + local), 2 * (left * EXP_DEV + pick[left]) + 1)
    order = jnp.argsort(order_key).astype(jnp.int32)
    hot_slot = jax.random.randint(jax.random.fold_in(key, 12), (), 0, virtual)
    many = virtual // 4
    total = TOK_DEV * TOP
    rest = total - many * CAP
    cold = virtual - many

    def block(index):
        block_key = jax.random.fold_in(jax.random.fold_in(key, 13), index)
        scores = jax.random.permutation(jax.random.fold_in(block_key, 1), virtual).astype(jnp.int32)
        scores = jnp.where(labels == hot_slot, -1, scores)
        ranking = jnp.argsort(jnp.argsort(scores)).astype(jnp.int32)
        extra = (ranking - many < rest % cold).astype(jnp.int32)
        load = jnp.where(ranking < many, CAP, rest // cold + extra)
        ends = jnp.cumsum(load[order])
        position = jnp.arange(total, dtype=jnp.int32)
        which = jnp.sum((position[:, None] >= ends[None, :]).astype(jnp.int32), axis=1)
        listed = order[which].reshape(TOP, TOK_DEV)
        shuffle = jax.random.permutation(jax.random.fold_in(block_key, 2), TOK_DEV)
        return listed[:, shuffle].T
    blocks = jax.vmap(block)(jnp.arange(N_EXPERT, dtype=jnp.int32))
    return blocks.reshape(TOKENS, TOP).astype(jnp.int32)


def levels(own_key, extent, cuts, smallest, top_value):
    loudness = 1.0
    for dim, shards_of in cuts:
        draws = jax.random.uniform(jax.random.fold_in(jax.random.fold_in(own_key, 6), dim), (shards_of,), jnp.float32, smallest / len(cuts), top_value / len(cuts))
        loudness = loudness * jnp.repeat(jnp.exp(draws), extent[dim] // shards_of).reshape((-1,) + (1,) * (len(extent) - 1 - dim))
    return loudness


def centred(stream_key, extent, deviation, reach, cuts=(), kind=jnp.bfloat16):
    result = deviation * jax.random.normal(stream_key, extent, jnp.float32)
    if cuts:
        result = result * levels(stream_key, extent, cuts, -0.22, 0.18)
    return jnp.clip(result, -reach, reach).astype(kind)


def setup_inputs(seed: int = 0, part: int = 0) -> dict:
    key_list = jax.random.split(jax.random.key(seed), 8)
    part_keys = jax.random.split(jax.random.fold_in(key_list[7], part), 8)
    tokens = centred(part_keys[0], (TOKENS, D), 1.0, 6.0, ((0, 16),))
    target = draw_target(jax.random.fold_in(jax.random.fold_in(key_list[7], part), 71), part)
    router_weight = jnp.clip(jnp.exp(math.log(1.0) - 2.3025851 * jax.random.uniform(part_keys[2], (TOKENS, TOP), jnp.float32) ** levels(part_keys[2], (TOKENS, TOP), ((0, 16),), -0.2, 0.2)), 0.1, 1.0)
    replica_pick = draw_replica_pick(jax.random.fold_in(jax.random.fold_in(key_list[7], part), 71), part)
    w_gate = centred(key_list[4], (EXPERTS, D, FF), D ** -0.5, 0.125, ((0, 16),))
    w_up = centred(key_list[5], (EXPERTS, D, FF), D ** -0.5, 0.125, ((0, 16),))
    w_down = centred(key_list[6], (EXPERTS, FF, D), FF ** -0.5, 0.21875, ((0, 16),))
    return dict(tokens=tokens, target=target, router_weight=router_weight, replica_pick=replica_pick, w_gate=w_gate, w_up=w_up, w_down=w_down)


def reference(tokens, target, router_weight, replica_pick, w_gate, w_up, w_down):
    slots = EXP_DEV + 1
    host = target // slots
    local = target % slots
    left = (host - 1) % N_EXPERT
    expert_id = jnp.where(local < EXP_DEV, host * EXP_DEV + local, left * EXP_DEV + replica_pick[left]).astype(jnp.int32)
    share = router_weight / jnp.sum(router_weight, axis=1, keepdims=True)

    def step(total, item):
        weight_gate, weight_up, weight_down, which = item
        coeff = jnp.sum(jnp.where(expert_id == which, share, jnp.zeros_like(share)), axis=1)
        gate = jnp.dot(tokens, weight_gate, preferred_element_type=jnp.float32)
        upper = jnp.dot(tokens, weight_up, preferred_element_type=jnp.float32)
        hidden = (jax.nn.silu(gate) * upper).astype(jnp.bfloat16)
        output = jnp.dot(hidden, weight_down, preferred_element_type=jnp.float32).astype(jnp.bfloat16)
        return total + coeff[:, None] * output.astype(total.dtype), None

    start = jnp.zeros((TOKENS, D), jnp.float32)
    total, unused = lax.scan(step, start, (w_gate, w_up, w_down, jnp.arange(EXPERTS, dtype=jnp.int32)))
    return total.astype(jnp.bfloat16)
```

```python
import jax
import jax.numpy as jnp
from jax import lax
from jax.sharding import PartitionSpec as P


def body(tokens, target, router_weight, replica_pick, w_gate, w_up, w_down):
    tok_rows, width = tokens.shape
    per_device = w_gate.shape[0]
    slots = per_device + 1
    groups = lax.axis_size("expert")
    me = lax.axis_index("expert")
    share = router_weight / jnp.sum(router_weight, axis=1, keepdims=True)
    all_tokens = lax.all_gather(tokens, "expert", axis=0, tiled=True)
    all_target = lax.all_gather(target, "expert", axis=0, tiled=True)
    all_share = lax.all_gather(share, "expert", axis=0, tiled=True)
    lent = replica_pick[0]
    away = lax.rem(me + 1, groups) * slots + per_device
    parts = []
    for local in range(per_device):
        hit = all_target == me * slots + local
        hit = hit | ((all_target == away) & (lent == local))
        coeff = jnp.sum(jnp.where(hit, all_share, 0.0), axis=1, keepdims=True)
        gate = jnp.dot(all_tokens, w_gate[local], preferred_element_type=jnp.float32)
        upper = jnp.dot(all_tokens, w_up[local], preferred_element_type=jnp.float32)
        parts.append((jax.nn.silu(gate) * upper * coeff).astype(jnp.bfloat16))
    hidden = jnp.concatenate(parts, axis=1)
    down = w_down.reshape(-1, width)
    partial = jnp.dot(hidden, down, preferred_element_type=jnp.float32).astype(jnp.bfloat16)
    return lax.psum_scatter(partial, "expert", scatter_dimension=0, tiled=True)


def solution(mesh):
    in_specs = (
        P(("dp", "expert"), None),
        P(("dp", "expert"), None),
        P(("dp", "expert"), None),
        P(("dp", "expert")),
        P("expert", None, None),
        P("expert", None, None),
        P("expert", None, None),
    )
    out_specs = P(("dp", "expert"), None)
    return jax.shard_map(body, mesh=mesh, in_specs=in_specs, out_specs=out_specs, check_vma=False)
```

```python
import jax
import jax.numpy as jnp
from jax import lax
from jax.sharding import PartitionSpec as P

CHUNKS = 2


def body(tokens, target, router_weight, replica_pick, w_gate, w_up, w_down):
    tok_rows, width = tokens.shape
    per_device = w_gate.shape[0]
    slots = per_device + 1
    groups = lax.axis_size("expert")
    me = lax.axis_index("expert")
    share = router_weight / jnp.sum(router_weight, axis=1, keepdims=True)
    step = tok_rows // CHUNKS
    gathered = [
        lax.all_gather(tokens[c * step:(c + 1) * step], "expert", axis=0, tiled=True)
        for c in range(CHUNKS)
    ]
    all_target = lax.all_gather(target, "expert", axis=0)
    all_share = lax.all_gather(share, "expert", axis=0)
    lent = replica_pick[0]
    away = lax.rem(me + 1, groups) * slots + per_device
    down = w_down.reshape(-1, width)
    outs = []
    for c in range(CHUNKS):
        rows = gathered[c]
        parts = []
        for local in range(per_device):
            hit = all_target == me * slots + local
            hit = hit | ((all_target == away) & (lent == local))
            coeff = jnp.sum(jnp.where(hit, all_share, 0.0), axis=2)
            coeff = coeff[:, c * step:(c + 1) * step].reshape(-1, 1)
            gate = jnp.dot(rows, w_gate[local], preferred_element_type=jnp.float32)
            upper = jnp.dot(rows, w_up[local], preferred_element_type=jnp.float32)
            parts.append((jax.nn.silu(gate) * upper * coeff).astype(jnp.bfloat16))
        hidden = jnp.concatenate(parts, axis=1)
        partial = jnp.dot(hidden, down, preferred_element_type=jnp.float32).astype(jnp.bfloat16)
        outs.append(lax.psum_scatter(partial, "expert", scatter_dimension=0, tiled=True))
    return jnp.concatenate(outs, axis=0)


def solution(mesh):
    in_specs = (
        P(("dp", "expert"), None),
        P(("dp", "expert"), None),
        P(("dp", "expert"), None),
        P(("dp", "expert")),
        P("expert", None, None),
        P("expert", None, None),
        P("expert", None, None),
    )
    out_specs = P(("dp", "expert"), None)
    return jax.shard_map(body, mesh=mesh, in_specs=in_specs, out_specs=out_specs, check_vma=False)
```

```python
import functools

import jax
import jax.numpy as jnp
from jax import lax
from jax.experimental import pallas as pl
from jax.experimental.pallas import tpu as pltpu
from jax.sharding import PartitionSpec as P

SIDE = 4
CHUNKS = 2
GROUP = 4
DIRS = ((0, 1), (0, -1), (1, 0), (-1, 0))
K1, K2, K3, K4A, K4B, K5, K7, K6A, K6B, K8 = range(10)
FULL = {K1: 0, K2: 1, K4A: 2, K4B: 3, K7: 4}
HALF = {K3: 0, K5: 1, K6A: 2, K6B: 3, K8: 4}
ORDER = (
    (0, 0), (0, 1), (0, 3), (1, 0),
    (3, 0), (1, 1), (1, 3), (3, 1),
    (3, 3), (0, 2), (2, 0), (1, 2),
    (3, 2), (2, 1), (2, 3), (2, 2),
)
WHERE = {offset: place for place, offset in enumerate(ORDER)}


def plus(a, b, scale=1):
    return ((a[0] + scale * b[0]) % SIDE, (a[1] + scale * b[1]) % SIDE)


def block_of(kind, d, rows):
    along_x = d[0] == 0
    first = 0 if along_x else 1
    other = 1 - first
    w = (1, 0) if along_x else (0, 1)
    zero = (0, 0)
    back = plus(zero, d, -1)
    whole = (0, rows)
    part = (0, rows // 2) if d[0] + d[1] > 0 else (rows // 2, rows // 2)
    return {
        K1: (first, zero, whole),
        K2: (other, zero, whole),
        K3: (first, back, part),
        K4A: (other, plus(zero, w), whole),
        K4B: (other, plus(zero, w, -1), whole),
        K5: (other, back, part),
        K7: (other, plus(zero, w, 2), whole),
        K6A: (other, plus(w, d, -1), part),
        K6B: (other, plus(plus(zero, w, -1), d, -1), part),
        K8: (other, plus(plus(zero, w, 2), d, -1), part),
    }[kind]


def kernel(
    tokens, target, weight, lent, w_gate, w_up, w_down, out,
    buf, wg, wu, wd, hid, coef, sh_out, sh_in, rfull, rhalf,
    wsem, tsem, osem, ag_send, ag_recv, rs_send, rs_recv, sh_send, sh_recv,
):
    dp = lax.axis_index("dp")
    me = lax.axis_index("expert")
    my_z, my_x = me // SIDE, me % SIDE
    experts, width, ff = w_gate.shape
    rows = tokens.shape[0] // CHUNKS
    half = width // 2
    tile = 256 if ff % 256 == 0 else 128
    wide = 512 if width % 512 == 0 else 128
    hidden_tiles = experts * ff // tile
    out_tiles = width // wide
    steps = hidden_tiles + out_tiles
    group_rows = GROUP * rows
    groups = CHUNKS * len(ORDER) // GROUP

    def at(offset):
        z = lax.rem(my_z + offset[0] + SIDE, SIDE)
        x = lax.rem(my_x + offset[1] + SIDE, SIDE)
        return z * SIDE + x

    def device(offset):
        return (dp, at(offset))

    def region(b, h, offset, part):
        start = WHERE[offset] * rows + part[0]
        return buf.at[b, pl.ds(start, part[1]), pl.ds(h * half, half)]

    def gather_copy(c, kind, n):
        d = DIRS[n]
        h, q, part = block_of(kind, d, rows)
        return pltpu.make_async_remote_copy(
            src_ref=region(c, h, q, part),
            dst_ref=region(c, h, plus(q, d, -1), part),
            send_sem=ag_send.at[c, kind, n],
            recv_sem=ag_recv.at[c, kind, n],
            device_id=device(d),
            device_id_type=pl.DeviceIdType.MESH,
        )

    def landing(c, kind, n):
        if kind in FULL:
            return rfull.at[c, FULL[kind], n]
        return rhalf.at[c, HALF[kind], n]

    def sum_buffer(c):
        return 2 - 2 * c

    def reduce_copy(c, kind, n):
        d = DIRS[n]
        h, q, part = block_of(kind, d, rows)
        return pltpu.make_async_remote_copy(
            src_ref=region(sum_buffer(c), h, plus(q, d, -1), part),
            dst_ref=landing(c, kind, n),
            send_sem=rs_send.at[c, kind, n],
            recv_sem=rs_recv.at[c, kind, n],
            device_id=device((-d[0], -d[1])),
            device_id_type=pl.DeviceIdType.MESH,
        )

    def start(make, c, kinds):
        for kind in kinds:
            for n in range(4):
                make(c, kind, n).start()

    def arrive(make, c, kinds):
        for kind in kinds:
            for n in range(4):
                make(c, kind, n).wait_recv()

    def sent(make, c):
        for kind in range(10):
            for n in range(4):
                make(c, kind, n).wait_send()

    def add(c, pairs):
        where = {}
        for kind, n in pairs:
            h, q, part = block_of(kind, DIRS[n], rows)
            where.setdefault((h, q, part), []).append(landing(c, kind, n))
        b = sum_buffer(c)
        for (h, q, part), sources in where.items():
            base = WHERE[q] * rows + part[0]
            cols = pl.ds(h * half, half)

            @pl.loop(0, part[1] // 16)
            def _(r):
                spot = pl.ds(pl.multiple_of(base + r * 16, 16), 16)
                total = buf[b, spot, cols].astype(jnp.float32)
                for source in sources:
                    total += source[pl.ds(pl.multiple_of(r * 16, 16), 16), :].astype(jnp.float32)
                buf[b, spot, cols] = total.astype(jnp.bfloat16)

    everywhere = range(4)

    def each(*kinds):
        return [(kind, n) for kind in kinds for n in everywhere]

    def ag(c, stage):
        if stage == 0:
            start(gather_copy, c, (K1, K2))
        elif stage == 1:
            arrive(gather_copy, c, (K1,))
            start(gather_copy, c, (K3, K4A, K4B))
        elif stage == 2:
            arrive(gather_copy, c, (K2,))
            start(gather_copy, c, (K5,))
        elif stage == 3:
            arrive(gather_copy, c, (K3,))
            start(gather_copy, c, (K7,))
        elif stage == 4:
            arrive(gather_copy, c, (K4A, K4B))
            start(gather_copy, c, (K6A, K6B))
        elif stage == 5:
            arrive(gather_copy, c, (K5,))
        elif stage == 6:
            arrive(gather_copy, c, (K7,))
            start(gather_copy, c, (K8,))
        elif stage == 7:
            arrive(gather_copy, c, (K6A, K6B))
        elif stage == 8:
            arrive(gather_copy, c, (K8,))

    def rs(c, stage):
        if stage == 0:
            start(reduce_copy, c, (K8, K6A, K6B, K5))
        elif stage == 1:
            arrive(reduce_copy, c, (K8,))
            add(c, each(K8))
            start(reduce_copy, c, (K7,))
        elif stage == 2:
            arrive(reduce_copy, c, (K6A, K6B))
            add(c, each(K6A, K6B))
            start(reduce_copy, c, (K4A, K4B))
        elif stage == 3:
            arrive(reduce_copy, c, (K5,))
            add(c, each(K5))
            start(reduce_copy, c, (K2,))
        elif stage == 4:
            arrive(reduce_copy, c, (K7,))
            add(c, each(K7))
            start(reduce_copy, c, (K3,))
        elif stage == 5:
            arrive(reduce_copy, c, (K4A, K4B))
            add(c, each(K4A, K4B))
        elif stage == 6:
            arrive(reduce_copy, c, (K3,))
            add(c, each(K3))
            start(reduce_copy, c, (K1,))
        elif stage == 7:
            arrive(reduce_copy, c, (K2, K1))
            add(c, each(K2, K1))
            result(c).start()

    def result(c):
        return pltpu.make_async_copy(
            buf.at[sum_buffer(c), pl.ds(0, rows), :], out.at[pl.ds(c * rows, rows), :], osem.at[c]
        )

    def own(c):
        return pltpu.make_async_copy(
            tokens.at[pl.ds(c * rows, rows), :], buf.at[c, pl.ds(0, rows), :], tsem.at[c]
        )

    def weights():
        copies = []
        for e in range(experts):
            span = pl.ds(e * ff, ff)
            copies.append(pltpu.make_async_copy(w_gate.at[e], wg.at[:, span], wsem.at[0, e]))
            copies.append(pltpu.make_async_copy(w_up.at[e], wu.at[:, span], wsem.at[1, e]))
            copies.append(pltpu.make_async_copy(w_down.at[e], wd.at[span, :], wsem.at[2, e]))
        return copies

    def share_copy(offset):
        back = plus((0, 0), offset, -1)
        return pltpu.make_async_remote_copy(
            src_ref=sh_out.at[WHERE[offset]],
            dst_ref=sh_in.at[WHERE[back]],
            send_sem=sh_send.at[WHERE[offset]],
            recv_sem=sh_recv.at[WHERE[back]],
            device_id=device(offset),
            device_id_type=pl.DeviceIdType.MESH,
        )

    def share_arrival(offset):
        return share_copy(plus((0, 0), offset, -1))

    for c in range(CHUNKS):
        own(c).start()
    barrier = pltpu.get_barrier_semaphore()
    for offset in ORDER[1:]:
        pl.semaphore_signal(
            barrier, inc=1, device_id=device(offset), device_id_type=pl.DeviceIdType.MESH
        )
    choice = target[...]
    share = weight[...]
    share = share / jnp.sum(share, axis=0, keepdims=True)
    slots = experts + 1
    count = SIDE * SIDE
    for offset in ORDER:
        host = at(offset)
        named = [host * slots + k for k in range(experts)] + [lax.rem(host + 1, count) * slots + experts]
        for k, slot in enumerate(named):
            sh_out[WHERE[offset], k:k + 1, :] = jnp.sum(
                jnp.where(choice == slot, share, 0.0), axis=0, keepdims=True
            )
        for k in range(len(named), 8):
            sh_out[WHERE[offset], k:k + 1, :] = jnp.zeros((1, share.shape[1]), jnp.float32)
    for c in range(CHUNKS):
        own(c).wait()
    pl.semaphore_wait(barrier, len(ORDER) - 1)
    ag(0, 0)
    for copy in weights():
        copy.start()
    for offset in ORDER[1:]:
        share_copy(offset).start()
    sh_in[0] = sh_out[0]
    ag(0, 1)
    for offset in ORDER[1:]:
        share_arrival(offset).wait_recv()
    second = lent[0:1, :]
    for c in range(CHUNKS):
        span = pl.ds(c * rows, rows)
        for p in range(len(ORDER)):
            spare = sh_in[p, 2:3, span]
            sh_in[p, 0:1, span] = sh_in[p, 0:1, span] + (1.0 - second) * spare
            sh_in[p, 1:2, span] = sh_in[p, 1:2, span] + second * spare
        table = jnp.concatenate([sh_in[p, :, span] for p in range(len(ORDER))], axis=0)
        turned = jnp.transpose(table)
        for p in range(len(ORDER)):
            coef[pl.ds((c * len(ORDER) + p) * rows, rows), :] = turned[:, p * 8:p * 8 + 8]
    ag(0, 2)
    for copy in weights():
        copy.wait()

    events = {}

    def plan(g, j, fn, *args):
        events.setdefault(g * steps + min(j, steps - 1), []).append((fn, args))

    plan(0, 2, ag, 0, 3)
    plan(1, 0, ag, 0, 4)
    plan(1, 3, ag, 0, 5)
    plan(1, 8, ag, 0, 6)
    plan(1, 8, ag, 1, 0)
    plan(2, 0, ag, 0, 7)
    plan(2, 3, ag, 0, 8)
    plan(2, 8, ag, 1, 1)
    plan(3, 2, ag, 1, 2)
    plan(3, 4, ag, 1, 3)
    plan(4, 3, ag, 1, 4)
    plan(4, 6, sent, gather_copy, 0)
    plan(4, 6, ag, 1, 5)
    plan(5, 1, ag, 1, 6)
    plan(5, 1, rs, 0, 0)
    plan(5, 5, ag, 1, 7)
    plan(5, 8, ag, 1, 8)
    plan(6, 1, rs, 0, 1)
    plan(6, 5, rs, 0, 2)
    plan(6, 8, rs, 0, 3)
    plan(7, 2, rs, 0, 4)

    @pl.loop(0, groups * steps)
    def _(i):
        for when, calls in events.items():
            @pl.when(i == when)
            def _(calls=calls):
                for fn, args in calls:
                    fn(*args)
        g = i // steps
        j = i % steps
        c = g // (groups // CHUNKS)
        row0 = pl.multiple_of((g % (groups // CHUNKS)) * group_rows, group_rows)

        @pl.when(j < hidden_tiles)
        def _():
            cols = pl.ds(pl.multiple_of(j * tile, tile), tile)
            x = buf[c, pl.ds(row0, group_rows), :]
            gate = jnp.dot(x, wg[:, cols], preferred_element_type=jnp.float32)
            upper = jnp.dot(x, wu[:, cols], preferred_element_type=jnp.float32)
            both = coef[pl.ds(pl.multiple_of(g * group_rows, group_rows), group_rows), :]
            scale = jnp.where(j < hidden_tiles // experts, both[:, 0:1], both[:, 1:2])
            value = gate / (1.0 + jnp.exp(-gate)) * upper * scale
            hid[:, cols] = value.astype(jnp.bfloat16)

        @pl.when(j >= hidden_tiles)
        def _():
            cols = pl.ds(pl.multiple_of((j - hidden_tiles) * wide, wide), wide)
            y = jnp.dot(hid[...], wd[:, cols], preferred_element_type=jnp.float32)
            buf[2 - 2 * c, pl.ds(row0, group_rows), cols] = y.astype(jnp.bfloat16)

    rs(1, 0)
    rs(0, 5)
    rs(0, 6)
    rs(1, 1)
    rs(1, 2)
    rs(1, 3)
    rs(0, 7)
    rs(1, 4)
    rs(1, 5)
    rs(1, 6)
    rs(1, 7)
    for c in range(CHUNKS):
        result(c).wait()
    sent(gather_copy, 1)
    sent(reduce_copy, 0)
    sent(reduce_copy, 1)
    for offset in ORDER[1:]:
        share_copy(offset).wait_send()


def body(tokens, target, router_weight, replica_pick, w_gate, w_up, w_down):
    tok_rows, width = tokens.shape
    experts, _, ff = w_gate.shape
    rows = tok_rows // CHUNKS
    count = SIDE * SIDE
    lent = jnp.broadcast_to(replica_pick.astype(jnp.float32)[:, None], (8, rows))
    any_space = pl.BlockSpec(memory_space=pl.ANY)
    vmem = pl.BlockSpec(memory_space=pltpu.VMEM)
    dma = pltpu.SemaphoreType.DMA
    moved = 30 * rows * width
    return pl.pallas_call(
        kernel,
        out_shape=jax.ShapeDtypeStruct((tok_rows, width), jnp.bfloat16),
        in_specs=[any_space, vmem, vmem, vmem, any_space, any_space, any_space],
        out_specs=any_space,
        scratch_shapes=[
            pltpu.VMEM((3, count * rows, width), jnp.bfloat16),
            pltpu.VMEM((width, experts * ff), jnp.bfloat16),
            pltpu.VMEM((width, experts * ff), jnp.bfloat16),
            pltpu.VMEM((experts * ff, width), jnp.bfloat16),
            pltpu.VMEM((GROUP * rows, experts * ff), jnp.bfloat16),
            pltpu.VMEM((count * tok_rows, 8), jnp.float32),
            pltpu.VMEM((count, 8, tok_rows), jnp.float32),
            pltpu.VMEM((count, 8, tok_rows), jnp.float32),
            pltpu.VMEM((CHUNKS, len(FULL), 4, rows, width // 2), jnp.bfloat16),
            pltpu.VMEM((CHUNKS, len(HALF), 4, rows // 2, width // 2), jnp.bfloat16),
            dma((3, experts)),
            dma((CHUNKS,)),
            dma((CHUNKS,)),
            dma((CHUNKS, 10, 4)),
            dma((CHUNKS, 10, 4)),
            dma((CHUNKS, 10, 4)),
            dma((CHUNKS, 10, 4)),
            dma((count,)),
            dma((count,)),
        ],
        compiler_params=pltpu.CompilerParams(
            collective_id=0, has_side_effects=True, vmem_limit_bytes=67043328
        ),
        cost_estimate=pl.CostEstimate(
            flops=6 * count * tok_rows * width * ff * experts,
            bytes_accessed=3 * experts * width * ff * 2,
            transcendentals=count * tok_rows * ff * experts,
        ),
        name="moe_layer",
    )(tokens, target.T, router_weight.T, lent, w_gate, w_up, w_down)


def solution(mesh):
    in_specs = (
        P(("dp", "expert"), None),
        P(("dp", "expert"), None),
        P(("dp", "expert"), None),
        P(("dp", "expert")),
        P("expert", None, None),
        P("expert", None, None),
        P("expert", None, None),
    )
    out_specs = P(("dp", "expert"), None)
    return jax.shard_map(body, mesh=mesh, in_specs=in_specs, out_specs=out_specs, check_vma=False)
```

```python
import jax
import jax.numpy as jnp
from jax import lax
from jax.experimental import pallas as pl
from jax.experimental.pallas import tpu as pltpu
from jax.sharding import PartitionSpec as P

SIDE = 4
CHUNKS = 4
ORDER = tuple((dz, s) for s in range(2) for dz in range(SIDE))
WHERE = {offset: place for place, offset in enumerate(ORDER)}
UP, DOWN, OUTER = range(3)
STEP = {UP: 1, DOWN: -1}
Z_KINDS = ("Z1A", "Z1B", "Z2", "Z3A", "Z3B", "Z4")
O_KINDS = ("O1A", "O1B", "O3", "O4", "O5")
COPIES = tuple((k, n) for k in Z_KINDS for n in (UP, DOWN)) + tuple((k, OUTER) for k in O_KINDS)
INDEX = {copy: i for i, copy in enumerate(COPIES)}


def block_of(kind, n):
    if n == OUTER:
        return {
            "O1A": ("A", (0, 0), None), "O1B": ("B", (0, 0), None), "O3": ("B", (1, 0), None),
            "O4": ("B", (3, 0), None), "O5": ("B", (2, 0), None),
        }[kind]
    back = -STEP[n] % SIDE
    return {
        "Z1A": ("A", (0, 0), None), "Z1B": ("B", (0, 0), None), "Z2": ("A", (0, 1), None),
        "Z3A": ("A", (back, 0), n), "Z3B": ("B", (back, 0), n), "Z4": ("A", (back, 1), n),
    }[kind]


def moved(offset, n):
    if n == OUTER:
        return (offset[0], 1 - offset[1])
    return ((offset[0] - STEP[n]) % SIDE, offset[1])


SIZES = {}
SPOT = {}
for _copy in COPIES:
    _cols, _, _part = block_of(*_copy)
    _key = (_cols, _part is not None)
    SPOT[_copy] = (_key, SIZES.get(_key, 0))
    SIZES[_key] = SIZES.get(_key, 0) + 1
LANDINGS = tuple(sorted(SIZES))


def kernel(
    tokens, target, weight, lent, w_gate, w_up, w_down, out,
    buf, wg, wu, wd, hid, hid_two, coef, sh_out, sh_in, lent_in, land_a, land_b, land_c, land_d,
    wsem, tsem, osem, ag_send, ag_recv, rs_send, rs_recv, sh_send, sh_recv, ln_send, ln_recv,
    x_send, x_recv, y_send, y_recv, r_send, r_recv, c_send, c_recv,
):
    dp = lax.axis_index("dp")
    me = lax.axis_index("expert")
    my_z, my_x = me // SIDE, me % SIDE
    my_y, my_core = dp // 2, dp % 2
    experts, width, ff = w_gate.shape
    own = experts * ff
    rows = tokens.shape[0] // CHUNKS
    group = rows * len(ORDER)
    split = width // 128 * 9 // 16 * 128
    columns = {"A": (0, split), "B": (split, width - split)}
    landings = dict(zip(LANDINGS, (land_a, land_b, land_c, land_d)))
    tile = 256 if ff % 256 == 0 else 128
    wide = 512 if width % 512 == 0 else 128
    tiles = own // tile
    outs = width // wide
    inner_x = my_x + 1 - 2 * (my_x % 2)
    MESH = pl.DeviceIdType.MESH

    def host(offset, inner=False):
        z = lax.rem(my_z + offset[0], SIDE)
        x = my_x if offset[1] == 0 else SIDE - 1 - my_x
        if inner:
            x = x + 1 - 2 * (x % 2)
        return z * SIDE + x

    def device(offset):
        return (dp, host(offset))

    def toward(n):
        return device((0, 1)) if n == OUTER else device((STEP[n] % SIDE, 0))

    def back_from(n):
        return device((0, 1)) if n == OUTER else device((-STEP[n] % SIDE, 0))

    inner = (dp, my_z * SIDE + inner_x)
    cross = (dp + 1 - 2 * my_core, me)

    def plane(step):
        return lax.rem(my_y + step + SIDE, SIDE) * 2 + my_core

    def rows_of(c, offset, part):
        start = c * group + WHERE[offset] * rows
        if part is None:
            return start, rows
        return start + (0 if part == UP else rows // 2), rows // 2

    def region(c, cols, offset, part):
        start, size = rows_of(c, offset, part)
        return buf.at[pl.ds(start, size), pl.ds(*columns[cols])]

    def landing(c, copy):
        key, place = SPOT[copy]
        return landings[key].at[c, place]

    def gather_copy(c, copy):
        cols, q, part = block_of(*copy)
        n = copy[1]
        return pltpu.make_async_remote_copy(
            src_ref=region(c, cols, q, part), dst_ref=region(c, cols, moved(q, n), part),
            send_sem=ag_send.at[c, INDEX[copy]], recv_sem=ag_recv.at[c, INDEX[copy]],
            device_id=toward(n), device_id_type=MESH,
        )

    def reduce_copy(c, copy):
        cols, q, part = block_of(*copy)
        n = copy[1]
        return pltpu.make_async_remote_copy(
            src_ref=region(c, cols, moved(q, n), part), dst_ref=landing(c, copy),
            send_sem=rs_send.at[c, INDEX[copy]], recv_sem=rs_recv.at[c, INDEX[copy]],
            device_id=back_from(n), device_id_type=MESH,
        )

    def named(*kinds):
        return [copy for kind in kinds for copy in COPIES if copy[0] == kind]

    def start(make, c, *kinds):
        for copy in named(*kinds):
            make(c, copy).start()

    def arrive(make, c, *kinds):
        for copy in named(*kinds):
            make(c, copy).wait_recv()

    def sent(make, c):
        for copy in COPIES:
            make(c, copy).wait_send()

    def add(c, *kinds):
        where = {}
        for copy in named(*kinds):
            where.setdefault(block_of(*copy), []).append(landing(c, copy))
        for (cols, q, part), sources in where.items():
            base, size = rows_of(c, q, part)
            span = pl.ds(*columns[cols])

            @pl.loop(0, size // 16)
            def _(r):
                spot = pl.ds(pl.multiple_of(base + r * 16, 16), 16)
                total = buf[spot, span].astype(jnp.float32)
                for source in sources:
                    total += source[pl.ds(pl.multiple_of(r * 16, 16), 16), :].astype(jnp.float32)
                buf[spot, span] = total.astype(jnp.bfloat16)

    def ag(c, stage):
        if stage == 0:
            start(gather_copy, c, "Z1A", "Z1B", "O1A", "O1B")
        elif stage == 1:
            arrive(gather_copy, c, "O1A")
            start(gather_copy, c, "Z2")
        elif stage == 2:
            arrive(gather_copy, c, "Z1A", "Z1B")
            start(gather_copy, c, "O3", "O4", "Z3A", "Z3B")
        elif stage == 3:
            arrive(gather_copy, c, "Z2")
            start(gather_copy, c, "Z4")
        elif stage == 4:
            arrive(gather_copy, c, "Z3A", "Z3B")
            start(gather_copy, c, "O5")
        else:
            arrive(gather_copy, c, "O1B", "O3", "O4", "O5", "Z4")

    def rs(c, stage):
        if stage == 0:
            start(reduce_copy, c, "Z4", "Z3A", "O5", "O3", "O4", "O1B")
        elif stage == 1:
            arrive(reduce_copy, c, "Z4")
            add(c, "Z4")
            start(reduce_copy, c, "Z2")
        elif stage == 2:
            arrive(reduce_copy, c, "Z3A")
            add(c, "Z3A")
            start(reduce_copy, c, "Z1A")
        elif stage == 3:
            arrive(reduce_copy, c, "O5")
            add(c, "O5")
            start(reduce_copy, c, "Z3B")
        elif stage == 4:
            arrive(reduce_copy, c, "O3", "O4")
            add(c, "O3", "O4")
        elif stage == 5:
            arrive(reduce_copy, c, "Z3B")
            add(c, "Z3B")
            start(reduce_copy, c, "Z1B")
        elif stage == 6:
            arrive(reduce_copy, c, "Z2")
            add(c, "Z2")
            start(reduce_copy, c, "O1A")
        else:
            arrive(reduce_copy, c, "Z1A", "Z1B", "O1A", "O1B")
            add(c, "Z1A", "O1A", "Z1B", "O1B")
            result(c).start()

    def result(c):
        return pltpu.make_async_copy(
            buf.at[pl.ds(c * group, rows), :], out.at[pl.ds(c * rows, rows), :], osem.at[c]
        )

    def mine(c):
        return pltpu.make_async_copy(
            tokens.at[pl.ds(c * rows, rows), :], buf.at[pl.ds(c * group, rows), :], tsem.at[c]
        )

    def weights():
        copies = []
        for e in range(experts):
            span = pl.ds(e * ff, ff)
            copies.append(pltpu.make_async_copy(w_gate.at[e], wg.at[:, span], wsem.at[0, e]))
            copies.append(pltpu.make_async_copy(w_up.at[e], wu.at[:, span], wsem.at[1, e]))
            copies.append(pltpu.make_async_copy(w_down.at[e], wd.at[span, :], wsem.at[2, e]))
        return copies

    blocks = [(a, e) for a in range(3) for e in range(experts)]
    in_part, down_part = width // 8, ff // 8

    def slice_of(k, index):
        a, e = blocks[k]
        if a == 2:
            return wd.at[pl.ds(own + e * ff + index * down_part, down_part), :]
        return (wg, wu)[a].at[pl.ds(index * in_part, in_part), pl.ds(own + e * ff, ff)]

    def fetch(k):
        a, e = blocks[k]
        size = down_part if a == 2 else in_part
        return pltpu.make_async_remote_copy(
            src_ref=(w_gate, w_up, w_down)[a].at[e, pl.ds(dp * size, size), :], dst_ref=slice_of(k, dp),
            send_sem=x_send.at[k], recv_sem=x_recv.at[k], device_id=inner, device_id_type=MESH,
        )

    def spread(k, n):
        return pltpu.make_async_remote_copy(
            src_ref=slice_of(k, dp), dst_ref=slice_of(k, dp),
            send_sem=y_send.at[k, n], recv_sem=y_recv.at[k, n],
            device_id=(plane(STEP[n]), me), device_id_type=MESH,
        )

    def relay(k):
        n = UP if blocks[k][1] == 0 else DOWN
        source = plane(-STEP[n])
        return pltpu.make_async_remote_copy(
            src_ref=slice_of(k, source), dst_ref=slice_of(k, source),
            send_sem=r_send.at[k], recv_sem=r_recv.at[k],
            device_id=(plane(STEP[n]), me), device_id_type=MESH,
        )

    def across(k, m):
        source = plane((0, -1, 1, 2)[m])
        return pltpu.make_async_remote_copy(
            src_ref=slice_of(k, source), dst_ref=slice_of(k, source),
            send_sem=c_send.at[k, m], recv_sem=c_recv.at[k, m], device_id=cross, device_id_type=MESH,
        )

    def wx(k):
        fetch(k).wait_recv()
        spread(k, UP).start()
        spread(k, DOWN).start()
        across(k, 0).start()

    def wy(k):
        spread(k, UP).wait_recv()
        spread(k, DOWN).wait_recv()
        relay(k).start()
        across(k, 1).start()
        across(k, 2).start()

    def wr(k):
        relay(k).wait_recv()
        across(k, 3).start()

    def have(*ks):
        for k in ks:
            for m in range(4):
                across(k, m).wait_recv()

    def share_copy(offset):
        back = (-offset[0] % SIDE, offset[1])
        return pltpu.make_async_remote_copy(
            src_ref=sh_out.at[WHERE[offset]], dst_ref=sh_in.at[WHERE[back]],
            send_sem=sh_send.at[WHERE[offset]], recv_sem=sh_recv.at[WHERE[back]],
            device_id=device(offset), device_id_type=MESH,
        )

    def share_arrival(offset):
        return share_copy((-offset[0] % SIDE, offset[1]))

    lent_copy = pltpu.make_async_remote_copy(
        src_ref=lent, dst_ref=lent_in, send_sem=ln_send, recv_sem=ln_recv,
        device_id=inner, device_id_type=MESH,
    )

    for c in range(CHUNKS):
        mine(c).start()
    barrier = pltpu.get_barrier_semaphore()
    peers = [device(offset) for offset in ORDER[1:]]
    peers += [inner, cross, (plane(1), me), (plane(-1), me)]
    for peer in peers:
        pl.semaphore_signal(barrier, inc=1, device_id=peer, device_id_type=MESH)
    for c in range(CHUNKS):
        mine(c).wait()
    pl.semaphore_wait(barrier, len(peers))
    ag(0, 0)
    for k in range(len(blocks)):
        fetch(k).start()
    lent_copy.start()
    for copy in weights():
        copy.start()
    choice = target[...]
    share = weight[...]
    share = share / jnp.sum(share, axis=0, keepdims=True)
    slots = experts + 1
    count = SIDE * SIDE
    for offset in ORDER:
        row = 0
        for side in (False, True):
            place = host(offset, side)
            names = [place * slots + k for k in range(experts)]
            names.append(lax.rem(place + 1, count) * slots + experts)
            for slot in names:
                sh_out[WHERE[offset], row:row + 1, :] = jnp.sum(
                    jnp.where(choice == slot, share, 0.0), axis=0, keepdims=True
                )
                row += 1
        sh_out[WHERE[offset], row:8, :] = jnp.zeros((8 - row, share.shape[1]), jnp.float32)
    for offset in ORDER[1:]:
        share_copy(offset).start()
    sh_in[0] = sh_out[0]
    ag(0, 1)
    ag(0, 2)
    ag(0, 3)
    for offset in ORDER[1:]:
        share_arrival(offset).wait_recv()
    lent_copy.wait_recv()
    for p in range(len(ORDER)):
        for base, lend in ((0, lent), (3, lent_in)):
            second = lend[0:1, :]
            spare = sh_in[p, base + 2:base + 3, :]
            sh_in[p, base:base + 1, :] = sh_in[p, base:base + 1, :] + (1.0 - second) * spare
            sh_in[p, base + 1:base + 2, :] = sh_in[p, base + 1:base + 2, :] + second * spare
    both = 2 * rows
    for pair in range(CHUNKS // 2):
        table = jnp.concatenate([sh_in[p, :, pair * both:(pair + 1) * both] for p in range(len(ORDER))], axis=0)
        turned = jnp.transpose(table)
        for c in range(2):
            for p in range(len(ORDER)):
                base = (pair * 2 + c) * group + p * rows
                coef[base:base + rows, :] = turned[c * rows:(c + 1) * rows, p * 8:p * 8 + 8]
    wx(0)
    ag(0, 4)
    ag(1, 0)
    for copy in weights():
        copy.wait()
    ag(0, 5)

    def run(events, length, fn):
        @pl.loop(0, length)
        def _(i):
            for when in sorted(events):
                @pl.when(i == when)
                def _(calls=events[when]):
                    for call in calls:
                        call[0](*call[1:])
            fn(i)

    def hidden(first, second):
        def fn(i):
            g = first + i // tiles
            j = i % tiles
            cols = pl.ds(pl.multiple_of(j * tile + (own if second else 0), tile), tile)
            span = pl.ds(pl.multiple_of(g * group, group), group)
            x = buf[span, :]
            gate = jnp.dot(x, wg[:, cols], preferred_element_type=jnp.float32)
            upper = jnp.dot(x, wu[:, cols], preferred_element_type=jnp.float32)
            part = coef[span, :]
            lane = 3 if second else 0
            scale = jnp.where(j < tiles // experts, part[:, lane:lane + 1], part[:, lane + 1:lane + 2])
            value = gate / (1.0 + jnp.exp(-gate)) * upper * scale
            to = pl.ds(pl.multiple_of(j * tile, tile), tile)
            if second:
                hid_two[g % 2, :, to] = value.astype(jnp.bfloat16)
            else:
                hid[span, to] = value.astype(jnp.bfloat16)
        return fn

    def outward(first):
        def fn(i):
            g = first + i // outs
            cols = pl.ds(pl.multiple_of((i % outs) * wide, wide), wide)
            span = pl.ds(pl.multiple_of(g * group, group), group)
            y = jnp.dot(hid[span, :], wd[0:own, cols], preferred_element_type=jnp.float32)
            y += jnp.dot(hid_two[g % 2], wd[own:2 * own, cols], preferred_element_type=jnp.float32)
            buf[span, cols] = y.astype(jnp.bfloat16)
        return fn

    def events(*rows_):
        table = {}
        for g, j, fn, *args in rows_:
            table.setdefault(g * tiles + min(j, tiles - 1), []).append((fn, *args))
        return table

    def out_events(*rows_):
        table = {}
        for g, j, fn, *args in rows_:
            table.setdefault(g * outs + min(j, outs - 1), []).append((fn, *args))
        return table

    run(events(
        (0, 3, wx, 1), (0, 3, wy, 0), (0, 3, ag, 1, 1), (0, 3, ag, 1, 2), (0, 5, ag, 1, 3),
        (1, 0, ag, 1, 4), (1, 0, ag, 2, 0), (1, 0, wx, 2), (1, 0, wy, 1), (1, 0, ag, 1, 5),
        (1, 3, ag, 2, 1), (1, 3, ag, 2, 2), (1, 5, ag, 2, 3), (1, 5, wx, 3), (1, 5, wr, 0),
        (2, 0, ag, 2, 4), (2, 0, ag, 3, 0), (2, 0, wy, 2), (2, 0, ag, 2, 5),
        (2, 2, wx, 4), (2, 2, wr, 1), (2, 3, ag, 3, 1), (2, 3, ag, 3, 2), (2, 5, ag, 3, 3),
        (3, 0, ag, 3, 4), (3, 0, wx, 5), (3, 0, wy, 3), (3, 0, ag, 3, 5),
        (3, 5, wr, 2), (3, 5, wr, 3),
    ), CHUNKS * tiles, hidden(0, False))
    have(0, 1, 2, 3)
    run(events((0, 4, wy, 4), (1, 4, wy, 5)), 2 * tiles, hidden(0, True))
    wr(4)
    wr(5)
    have(4, 5)
    sent(gather_copy, 0)
    sent(gather_copy, 1)
    run(out_events(
        (1, 0, rs, 0, 0), (1, 1, rs, 0, 1), (1, 2, rs, 0, 2), (1, 2, rs, 0, 3),
    ), 2 * outs, outward(0))
    rs(0, 6)
    rs(0, 4)
    rs(1, 0)
    sent(gather_copy, 2)
    run(events((0, 2, rs, 0, 5), (0, 4, rs, 0, 7), (0, 5, rs, 1, 1)), tiles, hidden(2, True))
    run(out_events(
        (0, 0, rs, 1, 2), (0, 0, rs, 1, 3), (0, 2, rs, 1, 6), (0, 2, rs, 1, 4),
    ), outs, outward(2))
    rs(2, 0)
    sent(gather_copy, 3)
    run(events(
        (0, 0, rs, 1, 5), (0, 2, rs, 1, 7), (0, 3, rs, 2, 1), (0, 4, rs, 2, 2), (0, 4, rs, 2, 3),
    ), tiles, hidden(3, True))
    run(out_events(
        (0, 0, rs, 2, 6), (0, 0, rs, 2, 4), (0, 2, rs, 2, 5),
    ), outs, outward(3))
    rs(3, 0)
    rs(2, 7)
    for stage in (1, 2, 3, 6, 4, 5, 7):
        rs(3, stage)
    for c in range(CHUNKS):
        result(c).wait()
        sent(reduce_copy, c)
    for offset in ORDER[1:]:
        share_copy(offset).wait_send()
    lent_copy.wait_send()
    for k in range(len(blocks)):
        fetch(k).wait_send()
        spread(k, UP).wait_send()
        spread(k, DOWN).wait_send()
        relay(k).wait_send()
        for m in range(4):
            across(k, m).wait_send()


def body(tokens, target, router_weight, replica_pick, w_gate, w_up, w_down):
    tok_rows, width = tokens.shape
    experts, _, ff = w_gate.shape
    rows = tok_rows // CHUNKS
    places = len(ORDER)
    own = experts * ff
    split = width // 128 * 9 // 16 * 128
    wide = {"A": split, "B": width - split}
    lent = jnp.broadcast_to(replica_pick.astype(jnp.float32)[:, None], (8, tok_rows))
    any_space = pl.BlockSpec(memory_space=pl.ANY)
    vmem = pl.BlockSpec(memory_space=pltpu.VMEM)
    dma = pltpu.SemaphoreType.DMA
    landings = [
        pltpu.VMEM((CHUNKS, SIZES[key], rows // 2 if key[1] else rows, wide[key[0]]), jnp.bfloat16)
        for key in LANDINGS
    ]
    return pl.pallas_call(
        kernel,
        out_shape=jax.ShapeDtypeStruct((tok_rows, width), jnp.bfloat16),
        in_specs=[any_space, vmem, vmem, vmem, any_space, any_space, any_space],
        out_specs=any_space,
        scratch_shapes=[
            pltpu.VMEM((CHUNKS * places * rows, width), jnp.bfloat16),
            pltpu.VMEM((width, 2 * own), jnp.bfloat16),
            pltpu.VMEM((width, 2 * own), jnp.bfloat16),
            pltpu.VMEM((2 * own, width), jnp.bfloat16),
            pltpu.VMEM((places * tok_rows, own), jnp.bfloat16),
            pltpu.VMEM((2, places * rows, own), jnp.bfloat16),
            pltpu.VMEM((places * tok_rows, 8), jnp.float32),
            pltpu.VMEM((places, 8, tok_rows), jnp.float32),
            pltpu.VMEM((places, 8, tok_rows), jnp.float32),
            pltpu.VMEM((8, tok_rows), jnp.float32),
            *landings,
            dma((3, experts)),
            dma((CHUNKS,)),
            dma((CHUNKS,)),
            dma((CHUNKS, len(COPIES))),
            dma((CHUNKS, len(COPIES))),
            dma((CHUNKS, len(COPIES))),
            dma((CHUNKS, len(COPIES))),
            dma((places,)),
            dma((places,)),
            dma,
            dma,
            dma((3 * experts,)),
            dma((3 * experts,)),
            dma((3 * experts, 2)),
            dma((3 * experts, 2)),
            dma((3 * experts,)),
            dma((3 * experts,)),
            dma((3 * experts, 4)),
            dma((3 * experts, 4)),
        ],
        compiler_params=pltpu.CompilerParams(
            collective_id=0, has_side_effects=True, vmem_limit_bytes=67043328
        ),
        cost_estimate=pl.CostEstimate(
            flops=12 * places * tok_rows * width * ff * experts,
            bytes_accessed=6 * experts * width * ff * 2,
            transcendentals=2 * places * tok_rows * ff * experts,
        ),
        name="moe_layer",
    )(tokens, target.T, router_weight.T, lent, w_gate, w_up, w_down)


def solution(mesh):
    in_specs = (
        P(("dp", "expert"), None),
        P(("dp", "expert"), None),
        P(("dp", "expert"), None),
        P(("dp", "expert")),
        P("expert", None, None),
        P("expert", None, None),
        P("expert", None, None),
    )
    out_specs = P(("dp", "expert"), None)
    return jax.shard_map(body, mesh=mesh, in_specs=in_specs, out_specs=out_specs, check_vma=False)
```

```python
import functools

import jax
import jax.numpy as jnp
from jax import lax
from jax.experimental import pallas as pl
from jax.experimental.pallas import tpu as pltpu
from jax.sharding import PartitionSpec as P

SIDE = 4
CHUNKS = 2
GROUP = 4
DIRS = ((0, 1), (0, -1), (1, 0), (-1, 0))
K1, K2, K3, K4A, K4B, K5, K7, K6A, K6B, K8 = range(10)
FULL = {K1: 0, K2: 1, K4A: 2, K4B: 3, K7: 4}
HALF = {K3: 0, K5: 1, K6A: 2, K6B: 3, K8: 4}
ORDER = (
    (0, 0), (0, 1), (0, 3), (1, 0),
    (3, 0), (1, 1), (1, 3), (3, 1),
    (3, 3), (0, 2), (2, 0), (1, 2),
    (3, 2), (2, 1), (2, 3), (2, 2),
)
WHERE = {offset: place for place, offset in enumerate(ORDER)}


def plus(a, b, scale=1):
    return ((a[0] + scale * b[0]) % SIDE, (a[1] + scale * b[1]) % SIDE)


def block_of(kind, d, rows):
    along_x = d[0] == 0
    first = 0 if along_x else 1
    other = 1 - first
    w = (1, 0) if along_x else (0, 1)
    zero = (0, 0)
    back = plus(zero, d, -1)
    whole = (0, rows)
    part = (0, rows // 2) if d[0] + d[1] > 0 else (rows // 2, rows // 2)
    return {
        K1: (first, zero, whole),
        K2: (other, zero, whole),
        K3: (first, back, part),
        K4A: (other, plus(zero, w), whole),
        K4B: (other, plus(zero, w, -1), whole),
        K5: (other, back, part),
        K7: (other, plus(zero, w, 2), whole),
        K6A: (other, plus(w, d, -1), part),
        K6B: (other, plus(plus(zero, w, -1), d, -1), part),
        K8: (other, plus(plus(zero, w, 2), d, -1), part),
    }[kind]


def kernel(
    tokens, target, weight, lent, w_gate, w_up, w_down, out,
    buf, wg, wu, wd, hid, coef, sh_out, sh_in, rfull, rhalf,
    wsem, tsem, osem, ag_send, ag_recv, rs_send, rs_recv, sh_send, sh_recv,
):
    dp = lax.axis_index("dp")
    me = lax.axis_index("expert")
    my_z, my_x = me // SIDE, me % SIDE
    experts, width, ff = w_gate.shape
    rows = tokens.shape[0] // CHUNKS
    half = width // 2
    tile = 256 if ff % 256 == 0 else 128
    wide = 512 if width % 512 == 0 else 128
    hidden_tiles = experts * ff // tile
    out_tiles = width // wide
    steps = hidden_tiles + out_tiles
    group_rows = GROUP * rows
    groups = CHUNKS * len(ORDER) // GROUP

    def at(offset):
        z = lax.rem(my_z + offset[0] + SIDE, SIDE)
        x = lax.rem(my_x + offset[1] + SIDE, SIDE)
        return z * SIDE + x

    def device(offset):
        return (dp, at(offset))

    def region(b, h, offset, part):
        start = WHERE[offset] * rows + part[0]
        return buf.at[b, pl.ds(start, part[1]), pl.ds(h * half, half)]

    def gather_copy(c, kind, n):
        d = DIRS[n]
        h, q, part = block_of(kind, d, rows)
        return pltpu.make_async_remote_copy(
            src_ref=region(c, h, q, part),
            dst_ref=region(c, h, plus(q, d, -1), part),
            send_sem=ag_send.at[c, kind, n],
            recv_sem=ag_recv.at[c, kind, n],
            device_id=device(d),
            device_id_type=pl.DeviceIdType.MESH,
        )

    def landing(c, kind, n):
        if kind in FULL:
            return rfull.at[c, FULL[kind], n]
        return rhalf.at[c, HALF[kind], n]

    def sum_buffer(c):
        return 2 - 2 * c

    def reduce_copy(c, kind, n):
        d = DIRS[n]
        h, q, part = block_of(kind, d, rows)
        return pltpu.make_async_remote_copy(
            src_ref=region(sum_buffer(c), h, plus(q, d, -1), part),
            dst_ref=landing(c, kind, n),
            send_sem=rs_send.at[c, kind, n],
            recv_sem=rs_recv.at[c, kind, n],
            device_id=device((-d[0], -d[1])),
            device_id_type=pl.DeviceIdType.MESH,
        )

    def start(make, c, kinds):
        for kind in kinds:
            for n in range(4):
                make(c, kind, n).start()

    def arrive(make, c, kinds):
        for kind in kinds:
            for n in range(4):
                make(c, kind, n).wait_recv()

    def sent(make, c):
        for kind in range(10):
            for n in range(4):
                make(c, kind, n).wait_send()

    def add(c, pairs):
        where = {}
        for kind, n in pairs:
            h, q, part = block_of(kind, DIRS[n], rows)
            where.setdefault((h, q, part), []).append(landing(c, kind, n))
        b = sum_buffer(c)
        for (h, q, part), sources in where.items():
            base = WHERE[q] * rows + part[0]
            cols = pl.ds(h * half, half)

            @pl.loop(0, part[1] // 32)
            def _(r):
                spot = pl.ds(pl.multiple_of(base + r * 32, 32), 32)
                total = buf[b, spot, cols].astype(jnp.float32)
                for source in sources:
                    total += source[pl.ds(pl.multiple_of(r * 32, 32), 32), :].astype(jnp.float32)
                buf[b, spot, cols] = total.astype(jnp.bfloat16)

    everywhere = range(4)

    def each(*kinds):
        return [(kind, n) for kind in kinds for n in everywhere]

    def ag(c, stage):
        if stage == 0:
            start(gather_copy, c, (K1, K2))
        elif stage == 1:
            arrive(gather_copy, c, (K1,))
            start(gather_copy, c, (K3, K4A, K4B))
        elif stage == 2:
            arrive(gather_copy, c, (K2,))
            start(gather_copy, c, (K5,))
        elif stage == 3:
            arrive(gather_copy, c, (K3,))
            start(gather_copy, c, (K7,))
        elif stage == 4:
            arrive(gather_copy, c, (K4A, K4B))
            start(gather_copy, c, (K6A, K6B))
        elif stage == 5:
            arrive(gather_copy, c, (K5,))
        elif stage == 6:
            arrive(gather_copy, c, (K7,))
            start(gather_copy, c, (K8,))
        elif stage == 7:
            arrive(gather_copy, c, (K6A, K6B))
        elif stage == 8:
            arrive(gather_copy, c, (K8,))

    def onward(c, kind, following):
        for n in everywhere:
            reduce_copy(c, kind, n).wait_recv()
            add(c, [(kind, n)])
            reduce_copy(c, following, n).start()

    def rs(c, stage):
        if stage == 0:
            start(reduce_copy, c, (K8, K6A, K6B, K5))
        elif stage == 1:
            onward(c, K8, K7)
        elif stage == 2:
            onward(c, K6A, K4A)
            onward(c, K6B, K4B)
        elif stage == 3:
            onward(c, K5, K2)
        elif stage == 4:
            for landed, freed in (((2, 3), (0, 1)), ((0, 1), (2, 3))):
                for n in landed:
                    reduce_copy(c, K7, n).wait_recv()
                add(c, [(K7, n) for n in landed])
                for n in freed:
                    reduce_copy(c, K3, n).start()
        elif stage == 5:
            arrive(reduce_copy, c, (K4A, K4B))
            add(c, each(K4A, K4B))
        elif stage == 6:
            onward(c, K3, K1)
        elif stage == 7:
            arrive(reduce_copy, c, (K2, K1))
            add(c, each(K2, K1))
            result(c).start()

    def result(c):
        return pltpu.make_async_copy(
            buf.at[sum_buffer(c), pl.ds(0, rows), :], out.at[pl.ds(c * rows, rows), :], osem.at[c]
        )

    def own(c):
        return pltpu.make_async_copy(
            tokens.at[pl.ds(c * rows, rows), :], buf.at[c, pl.ds(0, rows), :], tsem.at[c]
        )

    def weights():
        copies = []
        for e in range(experts):
            span = pl.ds(e * ff, ff)
            copies.append(pltpu.make_async_copy(w_gate.at[e], wg.at[:, span], wsem.at[0, e]))
            copies.append(pltpu.make_async_copy(w_up.at[e], wu.at[:, span], wsem.at[1, e]))
            copies.append(pltpu.make_async_copy(w_down.at[e], wd.at[span, :], wsem.at[2, e]))
        return copies

    def share_copy(offset):
        back = plus((0, 0), offset, -1)
        return pltpu.make_async_remote_copy(
            src_ref=sh_out.at[WHERE[offset]],
            dst_ref=sh_in.at[WHERE[back]],
            send_sem=sh_send.at[WHERE[offset]],
            recv_sem=sh_recv.at[WHERE[back]],
            device_id=device(offset),
            device_id_type=pl.DeviceIdType.MESH,
        )

    def share_arrival(offset):
        return share_copy(plus((0, 0), offset, -1))

    for c in range(CHUNKS):
        own(c).start()
    barrier = pltpu.get_barrier_semaphore()
    for offset in ORDER[1:]:
        pl.semaphore_signal(
            barrier, inc=1, device_id=device(offset), device_id_type=pl.DeviceIdType.MESH
        )
    for c in range(CHUNKS):
        own(c).wait()
    pl.semaphore_wait(barrier, len(ORDER) - 1)
    ag(0, 0)
    for copy in weights():
        copy.start()
    choice = target[...]
    share = weight[...]
    share = share / jnp.sum(share, axis=0, keepdims=True)
    slots = experts + 1
    count = SIDE * SIDE
    for offset in ORDER:
        host = at(offset)
        named = [host * slots + k for k in range(experts)] + [lax.rem(host + 1, count) * slots + experts]
        for k, slot in enumerate(named):
            sh_out[WHERE[offset], k:k + 1, :] = jnp.sum(
                jnp.where(choice == slot, share, 0.0), axis=0, keepdims=True
            )
        for k in range(len(named), 8):
            sh_out[WHERE[offset], k:k + 1, :] = jnp.zeros((1, share.shape[1]), jnp.float32)
    for offset in ORDER[1:]:
        share_copy(offset).start()
    sh_in[0] = sh_out[0]
    ag(0, 1)
    for offset in ORDER[1:]:
        share_arrival(offset).wait_recv()
    second = lent[0:1, :]
    for c in range(CHUNKS):
        span = pl.ds(c * rows, rows)
        for p in range(len(ORDER)):
            spare = sh_in[p, 2:3, span]
            sh_in[p, 0:1, span] = sh_in[p, 0:1, span] + (1.0 - second) * spare
            sh_in[p, 1:2, span] = sh_in[p, 1:2, span] + second * spare
        table = jnp.concatenate([sh_in[p, :, span] for p in range(len(ORDER))], axis=0)
        turned = jnp.transpose(table)
        for p in range(len(ORDER)):
            coef[pl.ds((c * len(ORDER) + p) * rows, rows), :] = turned[:, p * 8:p * 8 + 8]
    ag(0, 2)
    for copy in weights():
        copy.wait()

    events = {}

    def plan(g, j, fn, *args):
        events.setdefault(g * steps + min(j, steps - 1), []).append((fn, args))

    plan(0, 2, ag, 0, 3)
    plan(1, 0, ag, 0, 4)
    plan(1, 3, ag, 0, 5)
    plan(1, 8, ag, 0, 6)
    plan(1, 8, ag, 1, 0)
    plan(2, 0, ag, 0, 7)
    plan(2, 3, ag, 0, 8)
    plan(2, 8, ag, 1, 1)
    plan(3, 2, ag, 1, 2)
    plan(3, 4, ag, 1, 3)
    plan(4, 3, ag, 1, 4)
    plan(4, 6, sent, gather_copy, 0)
    plan(4, 6, ag, 1, 5)
    plan(5, 0, ag, 1, 6)
    plan(5, 0, rs, 0, 0)
    plan(5, 0, ag, 1, 7)
    plan(5, 8, ag, 1, 8)
    plan(6, 1, rs, 0, 1)
    plan(6, 5, rs, 0, 2)
    plan(6, 8, rs, 0, 3)
    plan(7, 0, rs, 1, 0)
    plan(7, 2, rs, 0, 4)

    @pl.loop(0, groups * steps)
    def _(i):
        for when, calls in events.items():
            @pl.when(i == when)
            def _(calls=calls):
                for fn, args in calls:
                    fn(*args)
        g = i // steps
        j = i % steps
        c = g // (groups // CHUNKS)
        turn = g % GROUP
        place = (1 - c) * turn + c * ((turn + 2) // 3 * (turn % 3 + 1))
        row0 = pl.multiple_of(place * group_rows, group_rows)

        @pl.when(j < hidden_tiles)
        def _():
            cols = pl.ds(pl.multiple_of(j * tile, tile), tile)
            x = buf[c, pl.ds(row0, group_rows), :]
            gate = jnp.dot(x, wg[:, cols], preferred_element_type=jnp.float32)
            upper = jnp.dot(x, wu[:, cols], preferred_element_type=jnp.float32)
            both = coef[pl.ds(pl.multiple_of((c * GROUP + place) * group_rows, group_rows), group_rows), :]
            scale = jnp.where(j < hidden_tiles // experts, both[:, 0:1], both[:, 1:2])
            value = gate / (1.0 + jnp.exp(-gate)) * upper * scale
            hid[:, cols] = value.astype(jnp.bfloat16)

        @pl.when(j >= hidden_tiles)
        def _():
            cols = pl.ds(pl.multiple_of((j - hidden_tiles) * wide, wide), wide)
            y = jnp.dot(hid[...], wd[:, cols], preferred_element_type=jnp.float32)
            buf[2 - 2 * c, pl.ds(row0, group_rows), cols] = y.astype(jnp.bfloat16)

    rs(0, 5)
    rs(0, 6)
    rs(1, 1)
    rs(1, 2)
    rs(1, 3)
    rs(0, 7)
    rs(1, 4)
    rs(1, 5)
    rs(1, 6)
    rs(1, 7)
    for c in range(CHUNKS):
        result(c).wait()
    sent(gather_copy, 1)
    sent(reduce_copy, 0)
    sent(reduce_copy, 1)
    for offset in ORDER[1:]:
        share_copy(offset).wait_send()


def body(tokens, target, router_weight, replica_pick, w_gate, w_up, w_down):
    tok_rows, width = tokens.shape
    experts, _, ff = w_gate.shape
    rows = tok_rows // CHUNKS
    count = SIDE * SIDE
    lent = jnp.broadcast_to(replica_pick.astype(jnp.float32)[:, None], (8, rows))
    any_space = pl.BlockSpec(memory_space=pl.ANY)
    vmem = pl.BlockSpec(memory_space=pltpu.VMEM)
    dma = pltpu.SemaphoreType.DMA
    moved = 30 * rows * width
    return pl.pallas_call(
        kernel,
        out_shape=jax.ShapeDtypeStruct((tok_rows, width), jnp.bfloat16),
        in_specs=[any_space, vmem, vmem, vmem, any_space, any_space, any_space],
        out_specs=any_space,
        scratch_shapes=[
            pltpu.VMEM((3, count * rows, width), jnp.bfloat16),
            pltpu.VMEM((width, experts * ff), jnp.bfloat16),
            pltpu.VMEM((width, experts * ff), jnp.bfloat16),
            pltpu.VMEM((experts * ff, width), jnp.bfloat16),
            pltpu.VMEM((GROUP * rows, experts * ff), jnp.bfloat16),
            pltpu.VMEM((count * tok_rows, 8), jnp.float32),
            pltpu.VMEM((count, 8, tok_rows), jnp.float32),
            pltpu.VMEM((count, 8, tok_rows), jnp.float32),
            pltpu.VMEM((CHUNKS, len(FULL), 4, rows, width // 2), jnp.bfloat16),
            pltpu.VMEM((CHUNKS, len(HALF), 4, rows // 2, width // 2), jnp.bfloat16),
            dma((3, experts)),
            dma((CHUNKS,)),
            dma((CHUNKS,)),
            dma((CHUNKS, 10, 4)),
            dma((CHUNKS, 10, 4)),
            dma((CHUNKS, 10, 4)),
            dma((CHUNKS, 10, 4)),
            dma((count,)),
            dma((count,)),
        ],
        compiler_params=pltpu.CompilerParams(
            collective_id=0, has_side_effects=True, vmem_limit_bytes=67043328
        ),
        cost_estimate=pl.CostEstimate(
            flops=6 * count * tok_rows * width * ff * experts,
            bytes_accessed=3 * experts * width * ff * 2,
            transcendentals=count * tok_rows * ff * experts,
        ),
        name="moe_layer",
    )(tokens, target.T, router_weight.T, lent, w_gate, w_up, w_down)


def solution(mesh):
    in_specs = (
        P(("dp", "expert"), None),
        P(("dp", "expert"), None),
        P(("dp", "expert"), None),
        P(("dp", "expert")),
        P("expert", None, None),
        P("expert", None, None),
        P("expert", None, None),
    )
    out_specs = P(("dp", "expert"), None)
    return jax.shard_map(body, mesh=mesh, in_specs=in_specs, out_specs=out_specs, check_vma=False)
```

```python
import functools

import jax
import jax.numpy as jnp
from jax import lax
from jax.experimental import pallas as pl
from jax.experimental.pallas import tpu as pltpu
from jax.sharding import PartitionSpec as P

SIDE = 4
CHUNKS = 2
GROUP = 4
DIRS = ((0, 1), (0, -1), (1, 0), (-1, 0))
K1, K2, K3, K4A, K4B, K5, K7, K6A, K6B, K8 = range(10)
FULL = {K1: 0, K2: 1, K4A: 2, K4B: 3, K7: 4}
HALF = {K3: 0, K5: 1, K6A: 2, K6B: 3, K8: 4}
ORDER = (
    (0, 0), (0, 1), (0, 3), (1, 0),
    (3, 0), (1, 1), (1, 3), (3, 1),
    (3, 3), (0, 2), (2, 0), (1, 2),
    (3, 2), (2, 1), (2, 3), (2, 2),
)
WHERE = {offset: place for place, offset in enumerate(ORDER)}


def plus(a, b, scale=1):
    return ((a[0] + scale * b[0]) % SIDE, (a[1] + scale * b[1]) % SIDE)


def block_of(kind, d, rows):
    along_x = d[0] == 0
    first = 0 if along_x else 1
    other = 1 - first
    w = (1, 0) if along_x else (0, 1)
    zero = (0, 0)
    back = plus(zero, d, -1)
    whole = (0, rows)
    part = (0, rows // 2) if d[0] + d[1] > 0 else (rows // 2, rows // 2)
    return {
        K1: (first, zero, whole),
        K2: (other, zero, whole),
        K3: (first, back, part),
        K4A: (other, plus(zero, w), whole),
        K4B: (other, plus(zero, w, -1), whole),
        K5: (other, back, part),
        K7: (other, plus(zero, w, 2), whole),
        K6A: (other, plus(w, d, -1), part),
        K6B: (other, plus(plus(zero, w, -1), d, -1), part),
        K8: (other, plus(plus(zero, w, 2), d, -1), part),
    }[kind]


def kernel(
    tokens, target, weight, lent, w_gate, w_up, w_down, out,
    buf, wg, wu, wd, hid, coef, sh_out, sh_in, rfull, rhalf,
    wsem, tsem, osem, ag_send, ag_recv, rs_send, rs_recv, sh_send, sh_recv,
):
    dp = lax.axis_index("dp")
    me = lax.axis_index("expert")
    my_z, my_x = me // SIDE, me % SIDE
    experts, width, ff = w_gate.shape
    rows = tokens.shape[0] // CHUNKS
    half = width // 2
    tile = 256 if ff % 256 == 0 else 128
    wide = 512 if width % 512 == 0 else 128
    hidden_tiles = experts * ff // tile
    out_tiles = width // wide
    steps = hidden_tiles + out_tiles
    group_rows = GROUP * rows
    groups = CHUNKS * len(ORDER) // GROUP

    def at(offset):
        z = lax.rem(my_z + offset[0] + SIDE, SIDE)
        x = lax.rem(my_x + offset[1] + SIDE, SIDE)
        return z * SIDE + x

    def device(offset):
        return (dp, at(offset))

    def region(b, h, offset, part):
        start = WHERE[offset] * rows + part[0]
        return buf.at[b, pl.ds(start, part[1]), pl.ds(h * half, half)]

    def gather_copy(c, kind, n):
        d = DIRS[n]
        h, q, part = block_of(kind, d, rows)
        return pltpu.make_async_remote_copy(
            src_ref=region(c, h, q, part),
            dst_ref=region(c, h, plus(q, d, -1), part),
            send_sem=ag_send.at[c, kind, n],
            recv_sem=ag_recv.at[c, kind, n],
            device_id=device(d),
            device_id_type=pl.DeviceIdType.MESH,
        )

    def landing(c, kind, n):
        if kind in FULL:
            return rfull.at[c, FULL[kind], n]
        return rhalf.at[c, HALF[kind], n]

    def sum_buffer(c):
        return 2 - 2 * c

    def reduce_copy(c, kind, n):
        d = DIRS[n]
        h, q, part = block_of(kind, d, rows)
        return pltpu.make_async_remote_copy(
            src_ref=region(sum_buffer(c), h, plus(q, d, -1), part),
            dst_ref=landing(c, kind, n),
            send_sem=rs_send.at[c, kind, n],
            recv_sem=rs_recv.at[c, kind, n],
            device_id=device((-d[0], -d[1])),
            device_id_type=pl.DeviceIdType.MESH,
        )

    def start(make, c, kinds):
        for kind in kinds:
            for n in range(4):
                make(c, kind, n).start()

    def arrive(make, c, kinds):
        for kind in kinds:
            for n in range(4):
                make(c, kind, n).wait_recv()

    def sent(make, c):
        for kind in range(10):
            for n in range(4):
                make(c, kind, n).wait_send()

    def add(c, pairs):
        where = {}
        for kind, n in pairs:
            h, q, part = block_of(kind, DIRS[n], rows)
            where.setdefault((h, q, part), []).append(landing(c, kind, n))
        b = sum_buffer(c)
        for (h, q, part), sources in where.items():
            base = WHERE[q] * rows + part[0]
            cols = pl.ds(h * half, half)

            @pl.loop(0, part[1] // 32)
            def _(r):
                spot = pl.ds(pl.multiple_of(base + r * 32, 32), 32)
                total = buf[b, spot, cols].astype(jnp.float32)
                for source in sources:
                    total += source[pl.ds(pl.multiple_of(r * 32, 32), 32), :].astype(jnp.float32)
                buf[b, spot, cols] = total.astype(jnp.bfloat16)

    everywhere = range(4)

    def each(*kinds):
        return [(kind, n) for kind in kinds for n in everywhere]

    def ag(c, stage):
        if stage == 0:
            start(gather_copy, c, (K1, K2))
        elif stage == 1:
            arrive(gather_copy, c, (K1,))
            start(gather_copy, c, (K3, K4A, K4B))
        elif stage == 2:
            arrive(gather_copy, c, (K2,))
            start(gather_copy, c, (K5,))
        elif stage == 3:
            arrive(gather_copy, c, (K3,))
            start(gather_copy, c, (K7,))
        elif stage == 4:
            arrive(gather_copy, c, (K4A, K4B))
            start(gather_copy, c, (K6A, K6B))
        elif stage == 5:
            arrive(gather_copy, c, (K5,))
        elif stage == 6:
            arrive(gather_copy, c, (K7,))
            start(gather_copy, c, (K8,))
        elif stage == 7:
            arrive(gather_copy, c, (K6A, K6B))
        elif stage == 8:
            arrive(gather_copy, c, (K8,))

    def onward(c, kind, following):
        for n in everywhere:
            reduce_copy(c, kind, n).wait_recv()
            add(c, [(kind, n)])
            reduce_copy(c, following, n).start()

    def rs(c, stage):
        if stage == 0:
            start(reduce_copy, c, (K8, K6A, K6B, K5))
        elif stage == 1:
            onward(c, K8, K7)
        elif stage == 2:
            onward(c, K6A, K4A)
            onward(c, K6B, K4B)
        elif stage == 3:
            onward(c, K5, K2)
        elif stage == 4:
            for landed, freed in (((2, 3), (0, 1)), ((0, 1), (2, 3))):
                for n in landed:
                    reduce_copy(c, K7, n).wait_recv()
                add(c, [(K7, n) for n in landed])
                for n in freed:
                    reduce_copy(c, K3, n).start()
        elif stage == 5:
            arrive(reduce_copy, c, (K4A, K4B))
            add(c, each(K4A, K4B))
        elif stage == 6:
            onward(c, K3, K1)
        elif stage == 7:
            arrive(reduce_copy, c, (K2, K1))
            add(c, each(K2, K1))
            result(c).start()

    def result(c):
        return pltpu.make_async_copy(
            buf.at[sum_buffer(c), pl.ds(0, rows), :], out.at[pl.ds(c * rows, rows), :], osem.at[c]
        )

    def own(c):
        return pltpu.make_async_copy(
            tokens.at[pl.ds(c * rows, rows), :], buf.at[c, pl.ds(0, rows), :], tsem.at[c]
        )

    def weights():
        copies = []
        for e in range(experts):
            span = pl.ds(e * ff, ff)
            copies.append(pltpu.make_async_copy(w_gate.at[e], wg.at[:, span], wsem.at[0, e]))
            copies.append(pltpu.make_async_copy(w_up.at[e], wu.at[:, span], wsem.at[1, e]))
            copies.append(pltpu.make_async_copy(w_down.at[e], wd.at[span, :], wsem.at[2, e]))
        return copies

    def share_copy(offset):
        back = plus((0, 0), offset, -1)
        return pltpu.make_async_remote_copy(
            src_ref=sh_out.at[WHERE[offset]],
            dst_ref=sh_in.at[WHERE[back]],
            send_sem=sh_send.at[WHERE[offset]],
            recv_sem=sh_recv.at[WHERE[back]],
            device_id=device(offset),
            device_id_type=pl.DeviceIdType.MESH,
        )

    def share_arrival(offset):
        return share_copy(plus((0, 0), offset, -1))

    for c in range(CHUNKS):
        own(c).start()
    barrier = pltpu.get_barrier_semaphore()
    for offset in ORDER[1:]:
        pl.semaphore_signal(
            barrier, inc=1, device_id=device(offset), device_id_type=pl.DeviceIdType.MESH
        )
    for c in range(CHUNKS):
        own(c).wait()
    pl.semaphore_wait(barrier, len(ORDER) - 1)
    ag(0, 0)
    for copy in weights():
        copy.start()
    choice = target[...]
    share = weight[...]
    share = share / jnp.sum(share, axis=0, keepdims=True)
    slots = experts + 1
    count = SIDE * SIDE
    for offset in ORDER:
        host = at(offset)
        named = [host * slots + k for k in range(experts)] + [lax.rem(host + 1, count) * slots + experts]
        for k, slot in enumerate(named):
            sh_out[WHERE[offset], k:k + 1, :] = jnp.sum(
                jnp.where(choice == slot, share, 0.0), axis=0, keepdims=True
            )
        for k in range(len(named), 8):
            sh_out[WHERE[offset], k:k + 1, :] = jnp.zeros((1, share.shape[1]), jnp.float32)
    for offset in ORDER[1:]:
        share_copy(offset).start()
    sh_in[0] = sh_out[0]
    ag(0, 1)
    for offset in ORDER[1:]:
        share_arrival(offset).wait_recv()
    second = lent[0:1, :]
    for c in range(CHUNKS):
        span = pl.ds(c * rows, rows)
        for p in range(len(ORDER)):
            spare = sh_in[p, 2:3, span]
            sh_in[p, 0:1, span] = sh_in[p, 0:1, span] + (1.0 - second) * spare
            sh_in[p, 1:2, span] = sh_in[p, 1:2, span] + second * spare
        table = jnp.concatenate([sh_in[p, :, span] for p in range(len(ORDER))], axis=0)
        turned = jnp.transpose(table)
        for p in range(len(ORDER)):
            coef[pl.ds((c * len(ORDER) + p) * rows, rows), :] = turned[:, p * 8:p * 8 + 8]
    ag(0, 2)
    for copy in weights():
        copy.wait()

    events = {}

    def plan(g, j, fn, *args):
        events.setdefault(g * steps + min(j, steps - 1), []).append((fn, args))

    plan(0, 2, ag, 0, 3)
    plan(1, 0, ag, 0, 4)
    plan(1, 3, ag, 0, 5)
    plan(1, 8, ag, 0, 6)
    plan(1, 8, ag, 1, 0)
    plan(2, 0, ag, 0, 7)
    plan(2, 3, ag, 0, 8)
    plan(2, 8, ag, 1, 1)
    plan(3, 2, ag, 1, 2)
    plan(3, 4, ag, 1, 3)
    plan(4, 3, ag, 1, 4)
    plan(4, 6, sent, gather_copy, 0)
    plan(4, 6, ag, 1, 5)
    plan(5, 0, ag, 1, 6)
    plan(5, 0, rs, 0, 0)
    plan(5, 0, ag, 1, 7)
    plan(5, 8, ag, 1, 8)
    plan(6, 1, rs, 0, 1)
    plan(6, 5, rs, 0, 2)
    plan(6, 8, rs, 0, 3)
    plan(7, 0, rs, 1, 0)
    plan(7, 2, rs, 0, 4)

    @pl.loop(0, groups * steps)
    def _(i):
        for when, calls in events.items():
            @pl.when(i == when)
            def _(calls=calls):
                for fn, args in calls:
                    fn(*args)
        g = i // steps
        j = i % steps
        c = g // (groups // CHUNKS)
        turn = g % GROUP
        place = (1 - c) * turn + c * ((turn + 2) // 3 * (turn % 3 + 1))
        row0 = pl.multiple_of(place * group_rows, group_rows)

        @pl.when(j < hidden_tiles)
        def _():
            cols = pl.ds(pl.multiple_of(j * tile, tile), tile)
            x = buf[c, pl.ds(row0, group_rows), :]
            gate = jnp.dot(x, wg[:, cols], preferred_element_type=jnp.float32)
            upper = jnp.dot(x, wu[:, cols], preferred_element_type=jnp.float32)
            both = coef[pl.ds(pl.multiple_of((c * GROUP + place) * group_rows, group_rows), group_rows), :]
            scale = jnp.where(j < hidden_tiles // experts, both[:, 0:1], both[:, 1:2])
            value = gate / (1.0 + jnp.exp(-gate)) * upper * scale
            hid[:, cols] = value.astype(jnp.bfloat16)

        @pl.when(j >= hidden_tiles)
        def _():
            cols = pl.ds(pl.multiple_of((j - hidden_tiles) * wide, wide), wide)
            y = jnp.dot(hid[...], wd[:, cols], preferred_element_type=jnp.float32)
            buf[2 - 2 * c, pl.ds(row0, group_rows), cols] = y.astype(jnp.bfloat16)

    rs(1, 1)
    rs(0, 5)
    rs(0, 6)
    rs(1, 2)
    rs(1, 3)
    rs(0, 7)
    rs(1, 4)
    rs(1, 5)
    rs(1, 6)
    rs(1, 7)
    for c in range(CHUNKS):
        result(c).wait()
    sent(gather_copy, 1)
    sent(reduce_copy, 0)
    sent(reduce_copy, 1)
    for offset in ORDER[1:]:
        share_copy(offset).wait_send()


def body(tokens, target, router_weight, replica_pick, w_gate, w_up, w_down):
    tok_rows, width = tokens.shape
    experts, _, ff = w_gate.shape
    rows = tok_rows // CHUNKS
    count = SIDE * SIDE
    lent = jnp.broadcast_to(replica_pick.astype(jnp.float32)[:, None], (8, rows))
    any_space = pl.BlockSpec(memory_space=pl.ANY)
    vmem = pl.BlockSpec(memory_space=pltpu.VMEM)
    dma = pltpu.SemaphoreType.DMA
    moved = 30 * rows * width
    return pl.pallas_call(
        kernel,
        out_shape=jax.ShapeDtypeStruct((tok_rows, width), jnp.bfloat16),
        in_specs=[any_space, vmem, vmem, vmem, any_space, any_space, any_space],
        out_specs=any_space,
        scratch_shapes=[
            pltpu.VMEM((3, count * rows, width), jnp.bfloat16),
            pltpu.VMEM((width, experts * ff), jnp.bfloat16),
            pltpu.VMEM((width, experts * ff), jnp.bfloat16),
            pltpu.VMEM((experts * ff, width), jnp.bfloat16),
            pltpu.VMEM((GROUP * rows, experts * ff), jnp.bfloat16),
            pltpu.VMEM((count * tok_rows, 8), jnp.float32),
            pltpu.VMEM((count, 8, tok_rows), jnp.float32),
            pltpu.VMEM((count, 8, tok_rows), jnp.float32),
            pltpu.VMEM((CHUNKS, len(FULL), 4, rows, width // 2), jnp.bfloat16),
            pltpu.VMEM((CHUNKS, len(HALF), 4, rows // 2, width // 2), jnp.bfloat16),
            dma((3, experts)),
            dma((CHUNKS,)),
            dma((CHUNKS,)),
            dma((CHUNKS, 10, 4)),
            dma((CHUNKS, 10, 4)),
            dma((CHUNKS, 10, 4)),
            dma((CHUNKS, 10, 4)),
            dma((count,)),
            dma((count,)),
        ],
        compiler_params=pltpu.CompilerParams(
            collective_id=0, has_side_effects=True, vmem_limit_bytes=67043328
        ),
        cost_estimate=pl.CostEstimate(
            flops=6 * count * tok_rows * width * ff * experts,
            bytes_accessed=3 * experts * width * ff * 2,
            transcendentals=count * tok_rows * ff * experts,
        ),
        name="moe_layer",
    )(tokens, target.T, router_weight.T, lent, w_gate, w_up, w_down)


def solution(mesh):
    in_specs = (
        P(("dp", "expert"), None),
        P(("dp", "expert"), None),
        P(("dp", "expert"), None),
        P(("dp", "expert")),
        P("expert", None, None),
        P("expert", None, None),
        P("expert", None, None),
    )
    out_specs = P(("dp", "expert"), None)
    return jax.shard_map(body, mesh=mesh, in_specs=in_specs, out_specs=out_specs, check_vma=False)
```
